32 devices in a mesh: parts: 2 (over y), space: 16 (over z, x, core).
Axes of the slice: x: 2, y: 2, z: 4, core: 2. Of those that a mesh axis runs over, the one named last changes fastest.
Arguments:
- snapshots: bfloat16 [2176, 8192], P('space', 'parts'), parts along dimension 1
- starts: int32 [16], replicated, may hold values from 0 to 1920, as said below
- bins: int32 [32], replicated, may hold values from 0 to 128
- mode_count: int32 [32], replicated, may hold values from 4 to 16
Outputs:
- modes: bfloat16 [32, 32, 8192], P(None, None, ('parts', 'space')), parts along dimension 2
- factor: float32 [64, 32, 32], P('parts'), parts along dimension 0
The draws below stay inside these ranges and needn't reach their ends.
There are 2 independent parts, one for each index of `parts`. The reference program is written for one: setup_inputs(seed, part) draws one part's arguments, and reference() takes and returns one part's arrays. A program takes and returns all parts, laid end to end along the dimension named above; an argument that names none is the same for every part. Nothing has to cross between parts.
Inputs may be any that keep to these rules, and one draw needn't show every extreme that they name: Block starts rise; the first block starts at 0, the last at 1920, and successive starts differ by 64 to 192 snapshots.
All inputs are finite; a program needn't handle non-finite values.
Results may differ from the reference program's by a relative error of at most 0.008.
Values may be sent and summed in bfloat16 or wider, within the bound.
No kernel may reach another device: no remote copies, remote signals or barrier semaphores. Data moves between devices by JAX's collectives and lax.ppermute only.
A program may use at most 64 MiB of HBM per device.

```python
import math
import jax
import jax.numpy as jnp
from jax import lax

NT = 2176
NB = 16
NWIN = 256
NFREQ = 32
P_SIZE = 4096


def draw_snapshots(key, part):
    key_noise = jax.random.fold_in(key, 101)
    key_rough = jax.random.fold_in(key, 202)
    position = jnp.arange(P_SIZE, dtype=jnp.float32) / P_SIZE
    ramp = 0.5 + position
    rough = jnp.exp(jax.random.uniform(key_rough, (P_SIZE,), jnp.float32, -0.35, 0.35))
    noise = jnp.clip(jax.random.normal(key_noise, (NT, P_SIZE), jnp.float32), -6.0, 6.0)
    return (noise * ramp[None, :] * rough[None, :]).astype(jnp.bfloat16)


def draw_starts(key, part):
    spacing = (NT - NWIN) // (NB - 1)
    reach = spacing // 4
    diagonal_shift = jax.random.randint(jax.random.fold_in(key, 505), (NB,), -reach, reach + 1)
    index = jnp.arange(NB, dtype=jnp.int32)
    middle = index * spacing + diagonal_shift
    first_fixed = jnp.where(index == 0, jnp.zeros_like(middle), middle)
    return jnp.where(index == NB - 1, jnp.full_like(middle, NT - NWIN), first_fixed).astype(jnp.int32)


def with_ends(entries, rng, least, high):
    place = [jax.random.randint(jax.random.fold_in(rng, axis), (), 0, length) for axis, length in enumerate(entries.shape)]
    widest = entries.shape.index(max(entries.shape))
    neighbour = place[:widest] + [(place[widest] + 1) % entries.shape[widest]] + place[widest + 1:]
    return entries.at[tuple(place)].set(least).at[tuple(neighbour)].set(high)


def setup_inputs(seed: int = 0, part: int = 0) -> dict:
    splits = jax.random.split(jax.random.key(seed), 5)
    part_splits = jax.random.split(jax.random.fold_in(splits[4], part), 5)
    return {
        "snapshots": draw_snapshots(jax.random.fold_in(jax.random.fold_in(splits[4], part), 71), part),
        "starts": draw_starts(jax.random.fold_in(splits[4], 71), part),
        "bins": with_ends(jax.random.randint(splits[2], (NFREQ,), 0, NWIN // 2 + 1), jax.random.fold_in(splits[2], 1), 0, (NWIN // 2 + 1) - 1).astype(jnp.int32),
        "mode_count": with_ends(jax.random.randint(splits[3], (NFREQ,), 4, NB + 1), jax.random.fold_in(splits[3], 1), 4, NB).astype(jnp.int32),
    }


def make_table(bins):
    offsets = jnp.arange(NWIN, dtype=jnp.int32)
    window = 0.5 - 0.5 * jnp.cos(2.0 * math.pi * offsets.astype(jnp.float32) / NWIN)
    scaling = 1.0 / jnp.sqrt(jnp.sum(window * window))
    turns = bins.astype(jnp.int32)[:, None] * offsets[None, :] % NWIN
    phases = 2.0 * math.pi * turns.astype(jnp.float32) / NWIN
    cos_rows = scaling * window[None, :] * jnp.cos(phases)
    sin_rows = -scaling * window[None, :] * jnp.sin(phases)
    return jnp.concatenate([cos_rows, sin_rows], axis=0).astype(jnp.bfloat16)

def reference(snapshots, starts, bins, mode_count):
    time_mean = lax.optimization_barrier(jnp.mean(snapshots.astype(jnp.float32), axis=0))
    centered = (snapshots.astype(jnp.float32) - time_mean[None, :]).astype(jnp.bfloat16)
    fourier_table = make_table(bins)

    def one_block(start):
        segment = lax.dynamic_slice_in_dim(centered, start.astype(jnp.int32), NWIN, 0)
        return jnp.dot(fourier_table.astype(jnp.float32), segment.astype(jnp.float32), preferred_element_type=jnp.float32).astype(jnp.bfloat16)
    spectra = lax.map(one_block, starts)
    real_component = jnp.transpose(spectra[:, :NFREQ, :], (1, 0, 2))
    imag_part = jnp.transpose(spectra[:, NFREQ:, :], (1, 0, 2))

    def single_frequency(inputs):
        real_rows, imag_rows, count = inputs
        stacked = jnp.concatenate([real_rows, imag_rows], axis=0)
        gram = jnp.dot(stacked.astype(jnp.float32), stacked.T.astype(jnp.float32), preferred_element_type=jnp.float32)
        real_real = gram[:NB, :NB]
        real_imag = gram[:NB, NB:]
        imag_real = gram[NB:, :NB]
        imag_imag = gram[NB:, NB:]
        summed = real_real + imag_imag
        skew_part = real_imag - imag_real
        upper_rows = jnp.concatenate([summed, -skew_part], axis=1)
        lower_rows = jnp.concatenate([skew_part, summed], axis=1)
        cross = jnp.concatenate([upper_rows, lower_rows], axis=0) / jnp.float32(P_SIZE)
        lower_cholesky_matrix = jnp.linalg.cholesky(cross)
        signed = jnp.concatenate([real_rows, -imag_rows], axis=0).astype(jnp.float32)
        basis = jax.scipy.linalg.solve_triangular(lower_cholesky_matrix, signed, lower=True)
        row_index = jnp.arange(2 * NB, dtype=jnp.int32) % NB
        keep = row_index[:, None] < count
        modes = jnp.where(keep, basis, jnp.zeros_like(basis)).astype(jnp.bfloat16)
        return (lower_cholesky_matrix.T, modes)
    factor, modes = lax.map(single_frequency, (real_component, imag_part, mode_count))
    return (modes, factor)
```

```python
import math

import jax
import jax.numpy as jnp
from jax import lax
from jax.experimental import pallas as pl
from jax.experimental.pallas import tpu as pltpu
from jax.sharding import PartitionSpec as P

NB = 16
NWIN = 256
NFREQ = 32
NROW = 2 * NB
SPAN = NWIN + 16
LANES = 128
PER = LANES // NROW
GROUPS = NFREQ // PER


def make_table(bins):
    offsets = jnp.arange(NWIN, dtype=jnp.int32)
    window = 0.5 - 0.5 * jnp.cos(2.0 * math.pi * offsets.astype(jnp.float32) / NWIN)
    scaling = 1.0 / jnp.sqrt(jnp.sum(window * window))
    turns = bins[:, None] * offsets[None, :] % NWIN
    phases = 2.0 * math.pi * turns.astype(jnp.float32) / NWIN
    cos_rows = scaling * window[None, :] * jnp.cos(phases)
    sin_rows = -scaling * window[None, :] * jnp.sin(phases)
    return jnp.concatenate([cos_rows, sin_rows], axis=0)


def shift_kernel(shift_ref, table_ref, out_ref):
    rows = 2 * NFREQ
    wide = jnp.concatenate([table_ref[...], jnp.zeros((rows, LANES), jnp.float32)], axis=1)
    for b in range(NB):
        out_ref[b * rows : (b + 1) * rows, :] = pltpu.roll(wide, shift_ref[b], 1).astype(jnp.bfloat16)


def shift_tables(shifts, table):
    return pl.pallas_call(
        shift_kernel,
        out_shape=jax.ShapeDtypeStruct((NB * 2 * NFREQ, NWIN + LANES), jnp.bfloat16),
        in_specs=[
            pl.BlockSpec(memory_space=pltpu.SMEM),
            pl.BlockSpec(memory_space=pltpu.VMEM),
        ],
        out_specs=pl.BlockSpec(memory_space=pltpu.VMEM),
    )(shifts, table)


def spectra_kernel(first_ref, series_ref, table_ref, spectra_ref, gram_ref, centered_ref, rows_ref):
    times, points = series_ref.shape
    rows = 2 * NFREQ
    step = 128
    total = jnp.zeros((8, points), jnp.float32)
    for t in range(0, times, step):
        part = series_ref[t : t + step, :].astype(jnp.float32)
        total = total + jnp.sum(part.reshape(step // 8, 8, points), axis=0)
    mean = jnp.sum(total, axis=0, keepdims=True) * (1.0 / times)
    for t in range(0, times, step):
        part = series_ref[t : t + step, :].astype(jnp.float32)
        centered_ref[t : t + step, :] = (part - mean).astype(jnp.bfloat16)
    for b in range(NB):
        first = pl.multiple_of(first_ref[b], 16)
        window = centered_ref[pl.ds(first, SPAN), :]
        product = jnp.dot(
            table_ref[b * rows : (b + 1) * rows, :SPAN], window, preferred_element_type=jnp.float32
        )
        for c in range(0, points, LANES):
            rows_ref[c // LANES, pl.ds(b, NFREQ, stride=NROW), :] = product[:NFREQ, c : c + LANES]
            rows_ref[c // LANES, pl.ds(NB + b, NFREQ, stride=NROW), :] = product[NFREQ:, c : c + LANES]
    lane = lax.broadcasted_iota(jnp.int32, (NB, LANES), 1)
    segment = lax.broadcasted_iota(jnp.int32, (NROW, LANES), 1) // NROW
    left = lane % NROW < NB
    for g in range(GROUPS):
        stacked = jnp.concatenate(
            [rows_ref[c, g * LANES : (g + 1) * LANES, :] for c in range(points // LANES)], axis=1
        ).astype(jnp.bfloat16)
        spectra_ref[g * LANES : (g + 1) * LANES, :] = stacked
        gram = lax.dot_general(
            stacked, stacked, (((1,), (1,)), ((), ())), preferred_element_type=jnp.float32
        )
        own = gram[:NROW]
        for k in range(1, PER):
            own = jnp.where(segment == k, gram[k * NROW : (k + 1) * NROW], own)
        lower = own[NB:]
        swapped = jnp.where(left, pltpu.roll(lower, LANES - NB, 1), pltpu.roll(lower, NB, 1))
        gram_ref[pl.ds(g, NB, stride=GROUPS), :] = own[:NB] + jnp.where(left, swapped, -swapped)


def spectra_and_gram(first, series, tables):
    times, points = series.shape
    return pl.pallas_call(
        spectra_kernel,
        out_shape=(
            jax.ShapeDtypeStruct((NFREQ * NROW, points), jnp.bfloat16),
            jax.ShapeDtypeStruct((NB * GROUPS, LANES), jnp.float32),
        ),
        in_specs=[
            pl.BlockSpec(memory_space=pltpu.SMEM),
            pl.BlockSpec(memory_space=pltpu.VMEM),
            pl.BlockSpec(memory_space=pltpu.VMEM),
        ],
        out_specs=(
            pl.BlockSpec(memory_space=pltpu.VMEM),
            pl.BlockSpec(memory_space=pltpu.VMEM),
        ),
        scratch_shapes=[
            pltpu.VMEM((times, points), jnp.bfloat16),
            pltpu.VMEM((points // LANES, NFREQ * NROW, LANES), jnp.float32),
        ],
    )(first, series, tables)


def modes_kernel(scale, gram_ref, spectra_ref, count_ref, modes_ref, factor_ref, upper_ref, inverse_ref):
    lane = lax.broadcasted_iota(jnp.int32, (GROUPS, LANES), 1)
    column = lane % NROW
    base = lane - column
    left = column < NB
    count = count_ref[...]
    matrix = [None] * NROW
    for i in range(NB):
        row = gram_ref[i * GROUPS : (i + 1) * GROUPS, :] * scale
        matrix[i] = jnp.where(left, row, -row)
        matrix[NB + i] = jnp.where(left, pltpu.roll(row, LANES - NB, 1), pltpu.roll(row, NB, 1))
    sign = jnp.where(left, 1.0, -1.0)
    inverse = [jnp.where(column == i, sign, 0.0) for i in range(NROW)]

    def spread(row, i):
        return jnp.take_along_axis(row, base + i, axis=1)

    for k in range(NROW):
        root = lax.rsqrt(spread(matrix[k], k))
        upper = matrix[k] * root
        done = inverse[k] * root
        upper_ref[k * GROUPS : (k + 1) * GROUPS, :] = jnp.where(column >= k, upper, 0.0)
        inverse_ref[k * GROUPS : (k + 1) * GROUPS, :] = jnp.where(count > k % NB, done, 0.0)
        for i in range(k + 1, NROW):
            along = spread(upper, i)
            matrix[i] = matrix[i] - along * upper
            inverse[i] = inverse[i] - along * done
    for g in range(GROUPS):
        upper = upper_ref[pl.ds(g, NROW, stride=GROUPS), :]
        for k in range(PER):
            factor_ref[g * PER + k, :, :] = upper[:, k * NROW : (k + 1) * NROW]
    segment = lax.broadcasted_iota(jnp.int32, (NROW, LANES), 1) // NROW
    for g in range(GROUPS):
        weights = inverse_ref[pl.ds(g, NROW, stride=GROUPS), :]
        blocks = jnp.concatenate([jnp.where(segment == k, weights, 0.0) for k in range(PER)], axis=0)
        high = blocks.astype(jnp.bfloat16)
        low = (blocks - high.astype(jnp.float32)).astype(jnp.bfloat16)
        values = spectra_ref[g * LANES : (g + 1) * LANES, :]
        product = jnp.dot(high, values, preferred_element_type=jnp.float32) + jnp.dot(
            low, values, preferred_element_type=jnp.float32
        )
        modes_ref[g * LANES : (g + 1) * LANES, :] = product.astype(jnp.bfloat16)


def modes_and_factor(gram, spectra, counts, all_points):
    points = spectra.shape[1]

    def kernel(*refs):
        modes_kernel(1.0 / all_points, *refs)

    return pl.pallas_call(
        kernel,
        out_shape=(
            jax.ShapeDtypeStruct((NFREQ * NROW, points), jnp.bfloat16),
            jax.ShapeDtypeStruct((NFREQ, NROW, NROW), jnp.float32),
        ),
        in_specs=[pl.BlockSpec(memory_space=pltpu.VMEM)] * 3,
        out_specs=(
            pl.BlockSpec(memory_space=pltpu.VMEM),
            pl.BlockSpec(memory_space=pltpu.VMEM),
        ),
        scratch_shapes=[pltpu.VMEM((NROW * GROUPS, LANES), jnp.float32)] * 2,
    )(gram, spectra, counts)


def sum_over_space(partial, groups):
    if groups & (groups - 1):
        return lax.psum(partial, "space")
    bit = 1
    while bit < groups:
        moves = [bit]
        if bit == 2 and 2 * bit < groups:
            moves = [bit, 2 * bit, 3 * bit]
        parts = [
            lax.ppermute(partial, "space", [(i, i ^ move) for i in range(groups)]) for move in moves
        ]
        for part in parts:
            partial = partial + part
        bit *= 2 if len(moves) == 1 else 4
    return partial


def on_device(snapshots, starts, bins, mode_count):
    time_dev, all_points = snapshots.shape
    groups = lax.axis_size("space")
    points_dev = all_points // groups
    times = time_dev * groups
    arranged = jnp.swapaxes(snapshots.reshape(time_dev, groups, points_dev), 0, 1)
    series = lax.all_to_all(arranged, "space", split_axis=0, concat_axis=0, tiled=True)
    series = series.reshape(times, points_dev)
    first = jnp.minimum(starts // 16 * 16, times - SPAN)
    tables = shift_tables(starts - first, make_table(bins))
    spectra, partial = spectra_and_gram(first, series, tables)
    gram = sum_over_space(partial, groups)
    counts = jnp.repeat(mode_count.reshape(GROUPS, PER), NROW, axis=1)
    modes, factor = modes_and_factor(gram, spectra, counts, all_points)
    return (modes.reshape(NFREQ, NROW, points_dev), factor)


def solution(mesh):
    in_specs = (P("space", "parts"), P(), P(), P())
    out_specs = (P(None, None, ("parts", "space")), P("parts", None, None))
    return jax.shard_map(
        on_device, mesh=mesh, in_specs=in_specs, out_specs=out_specs, check_vma=False
    )
```

```python
import math

import jax
import jax.numpy as jnp
from jax import lax
from jax.experimental import pallas as pl
from jax.experimental.pallas import tpu as pltpu
from jax.sharding import PartitionSpec as P

NB = 16
NWIN = 256
NFREQ = 32
NROW = 2 * NB
SPAN = NWIN + 16
LANES = 128
PER = LANES // NROW
GROUPS = NFREQ // PER
HALF = NB // 2
BLOCK = 4
VMEM = pltpu.CompilerParams(vmem_limit_bytes=16 * 1024 * 1024)


def make_table(bins):
    offsets = jnp.arange(NWIN, dtype=jnp.int32)
    window = 0.5 - 0.5 * jnp.cos(2.0 * math.pi * offsets.astype(jnp.float32) / NWIN)
    scaling = 1.0 / jnp.sqrt(jnp.sum(window * window))
    turns = bins[:, None] * offsets[None, :] % NWIN
    phases = 2.0 * math.pi * turns.astype(jnp.float32) / NWIN
    cos_rows = scaling * window[None, :] * jnp.cos(phases)
    sin_rows = -scaling * window[None, :] * jnp.sin(phases)
    return jnp.concatenate([cos_rows, sin_rows], axis=0)


def shift_kernel(shift_ref, table_ref, out_ref):
    rows = 2 * NFREQ
    wide = jnp.concatenate([table_ref[...], jnp.zeros((rows, LANES), jnp.float32)], axis=1)
    for b in range(NB):
        out_ref[b * rows : (b + 1) * rows, :] = pltpu.roll(wide, shift_ref[b], 1).astype(jnp.bfloat16)


def shift_tables(shifts, table):
    return pl.pallas_call(
        shift_kernel,
        out_shape=jax.ShapeDtypeStruct((NB * 2 * NFREQ, NWIN + LANES), jnp.bfloat16),
        in_specs=[
            pl.BlockSpec(memory_space=pltpu.SMEM),
            pl.BlockSpec(memory_space=pltpu.VMEM),
        ],
        out_specs=pl.BlockSpec(memory_space=pltpu.VMEM),
        compiler_params=VMEM,
    )(shifts, table)


def spectra_kernel(first_ref, series_ref, table_ref, spectra_ref, gram_ref, centered_ref, rows_ref):
    times, points = series_ref.shape
    rows = 2 * NFREQ
    step = 128
    total = jnp.zeros((8, points), jnp.float32)
    for t in range(0, times, step):
        part = series_ref[t : t + step, :].astype(jnp.float32)
        total = total + jnp.sum(part.reshape(step // 8, 8, points), axis=0)
    mean = jnp.sum(total, axis=0, keepdims=True) * (1.0 / times)
    for t in range(0, times, step):
        part = series_ref[t : t + step, :].astype(jnp.float32)
        centered_ref[t : t + step, :] = (part - mean).astype(jnp.bfloat16)
    for b in range(NB):
        first = pl.multiple_of(first_ref[b], 16)
        window = centered_ref[pl.ds(first, SPAN), :]
        product = jnp.dot(
            table_ref[b * rows : (b + 1) * rows, :SPAN], window, preferred_element_type=jnp.float32
        )
        for c in range(0, points, LANES):
            rows_ref[c // LANES, pl.ds(b, NFREQ, stride=NROW), :] = product[:NFREQ, c : c + LANES]
            rows_ref[c // LANES, pl.ds(NB + b, NFREQ, stride=NROW), :] = product[NFREQ:, c : c + LANES]
    lane = lax.broadcasted_iota(jnp.int32, (HALF, LANES), 1)
    segment = lax.broadcasted_iota(jnp.int32, (NROW, LANES), 1) // NROW
    left = lane % NROW < NB
    for g in range(GROUPS):
        stacked = jnp.concatenate(
            [rows_ref[c, g * LANES : (g + 1) * LANES, :] for c in range(points // LANES)], axis=1
        ).astype(jnp.bfloat16)
        spectra_ref[g * LANES : (g + 1) * LANES, :] = stacked
        gram = lax.dot_general(
            stacked, stacked, (((1,), (1,)), ((), ())), preferred_element_type=jnp.float32
        )
        own = gram[:NROW]
        for k in range(1, PER):
            own = jnp.where(segment == k, gram[k * NROW : (k + 1) * NROW], own)
        upper, lower = own[:NB], own[NB:]
        mixed = (upper - lower) + pltpu.roll(upper + lower, LANES - NB, 1)
        gram_ref[pl.ds(g, HALF, stride=GROUPS), :] = jnp.where(
            left, mixed[:HALF], pltpu.roll(mixed[HALF:], NB, 1)
        )


def spectra_and_gram(first, series, tables):
    times, points = series.shape
    return pl.pallas_call(
        spectra_kernel,
        out_shape=(
            jax.ShapeDtypeStruct((NFREQ * NROW, points), jnp.bfloat16),
            jax.ShapeDtypeStruct((HALF * GROUPS, LANES), jnp.float32),
        ),
        in_specs=[
            pl.BlockSpec(memory_space=pltpu.SMEM),
            pl.BlockSpec(memory_space=pltpu.VMEM),
            pl.BlockSpec(memory_space=pltpu.VMEM),
        ],
        out_specs=(
            pl.BlockSpec(memory_space=pltpu.VMEM),
            pl.BlockSpec(memory_space=pltpu.VMEM),
        ),
        scratch_shapes=[
            pltpu.VMEM((times, points), jnp.bfloat16),
            pltpu.VMEM((points // LANES, NFREQ * NROW, LANES), jnp.float32),
        ],
        compiler_params=VMEM,
    )(first, series, tables)


def unpack(packed):
    lane = lax.broadcasted_iota(jnp.int32, (GROUPS, LANES), 1)
    left = lane % NROW < NB
    rows = packed + [pltpu.roll(row, LANES - NB, 1) for row in packed]
    turned = list(rows)
    bit = 1
    while bit < NB:
        high = (lane & bit) != 0
        turned = [
            jnp.where(high, turned[i], pltpu.roll(turned[i - bit], LANES - bit, 1))
            if i & bit
            else jnp.where(high, pltpu.roll(turned[i + bit], bit, 1), turned[i])
            for i in range(NB)
        ]
        bit *= 2
    sums = [rows[i] + turned[i] for i in range(NB)]
    minus = [turned[i] - rows[i] for i in range(NB)]
    upper = [jnp.where(left, sums[i], pltpu.roll(minus[i], NB, 1)) for i in range(NB)]
    return upper + [pltpu.roll(row, NB, 1) for row in sums]


def modes_kernel(
    scale, gram_ref, other_ref, spectra_ref, count_ref, modes_ref, factor_ref, upper_ref, inverse_ref
):
    lane = lax.broadcasted_iota(jnp.int32, (GROUPS, LANES), 1)
    column = lane % NROW
    base = lane - column
    count = count_ref[...]
    matrix = unpack(
        [
            (gram_ref[r * GROUPS : (r + 1) * GROUPS, :] + other_ref[r * GROUPS : (r + 1) * GROUPS, :])
            * (0.5 * scale)
            for r in range(HALF)
        ]
    )
    sign = jnp.where(column < NB, 1.0, -1.0)
    inverse = [jnp.where(column == i, sign, 0.0) for i in range(NROW)]

    def spread(row, i):
        return jnp.take_along_axis(row, base + i, axis=1)

    for first in range(0, NROW, BLOCK):
        block = range(first, first + BLOCK)
        along = {(k, i): spread(matrix[k], i) for k in block for i in range(k, NROW)}
        scaled, solved = {}, {}
        for k in block:
            root = lax.rsqrt(along[k, k])
            upper_ref[k * GROUPS : (k + 1) * GROUPS, :] = jnp.where(column >= k, matrix[k] * root, 0.0)
            inverse_ref[k * GROUPS : (k + 1) * GROUPS, :] = jnp.where(count > k % NB, inverse[k] * root, 0.0)
            over = root * root
            scaled[k] = matrix[k] * over
            solved[k] = inverse[k] * over
            for p in range(k + 1, first + BLOCK):
                entry = along[k, p]
                matrix[p] = matrix[p] - entry * scaled[k]
                inverse[p] = inverse[p] - entry * solved[k]
                ratio = entry * over
                for i in range(p, NROW):
                    along[p, i] = along[p, i] - ratio * along[k, i]
        for i in range(first + BLOCK, NROW):
            for k in block:
                matrix[i] = matrix[i] - along[k, i] * scaled[k]
                inverse[i] = inverse[i] - along[k, i] * solved[k]
    for g in range(GROUPS):
        upper = upper_ref[pl.ds(g, NROW, stride=GROUPS), :]
        for k in range(PER):
            factor_ref[g * PER + k, :, :] = upper[:, k * NROW : (k + 1) * NROW]
    segment = lax.broadcasted_iota(jnp.int32, (NROW, LANES), 1) // NROW
    for g in range(GROUPS):
        weights = inverse_ref[pl.ds(g, NROW, stride=GROUPS), :]
        blocks = jnp.concatenate([jnp.where(segment == k, weights, 0.0) for k in range(PER)], axis=0)
        high = blocks.astype(jnp.bfloat16)
        low = (blocks - high.astype(jnp.float32)).astype(jnp.bfloat16)
        values = spectra_ref[g * LANES : (g + 1) * LANES, :]
        product = jnp.dot(high, values, preferred_element_type=jnp.float32) + jnp.dot(
            low, values, preferred_element_type=jnp.float32
        )
        modes_ref[g * LANES : (g + 1) * LANES, :] = product.astype(jnp.bfloat16)


def modes_and_factor(gram, other, spectra, counts, all_points):
    points = spectra.shape[1]

    def kernel(*refs):
        modes_kernel(1.0 / all_points, *refs)

    return pl.pallas_call(
        kernel,
        out_shape=(
            jax.ShapeDtypeStruct((NFREQ * NROW, points), jnp.bfloat16),
            jax.ShapeDtypeStruct((NFREQ, NROW, NROW), jnp.float32),
        ),
        in_specs=[pl.BlockSpec(memory_space=pltpu.VMEM)] * 4,
        out_specs=(
            pl.BlockSpec(memory_space=pltpu.VMEM),
            pl.BlockSpec(memory_space=pltpu.VMEM),
        ),
        scratch_shapes=[pltpu.VMEM((NROW * GROUPS, LANES), jnp.float32)] * 2,
        compiler_params=VMEM,
    )(gram, other, spectra, counts)


def sum_over_space(partial, groups):
    if groups & (groups - 1) or groups == 1:
        return lax.psum(partial, "space"), jnp.zeros_like(partial)
    bit, rounds = 1, []
    while bit < groups:
        if bit == 2 and 4 * bit < groups:
            rounds.append([bit, 2 * bit, 3 * bit])
            bit *= 4
        else:
            rounds.append([bit])
            bit *= 2
    for moves in rounds:
        parts = [
            lax.ppermute(partial, "space", [(i, i ^ move) for i in range(groups)]) for move in moves
        ]
        left, right = partial, parts[0]
        if len(moves) == 3:
            left, right = partial + parts[0], parts[1] + parts[2]
        partial = left + right
    return left, right


def on_device(snapshots, starts, bins, mode_count):
    time_dev, all_points = snapshots.shape
    groups = lax.axis_size("space")
    points_dev = all_points // groups
    times = time_dev * groups
    arranged = jnp.swapaxes(snapshots.reshape(time_dev, groups, points_dev), 0, 1)
    series = lax.all_to_all(arranged, "space", split_axis=0, concat_axis=0, tiled=True)
    series = series.reshape(times, points_dev)
    first = jnp.minimum(starts // 16 * 16, times - SPAN)
    tables = shift_tables(starts - first, make_table(bins))
    spectra, partial = spectra_and_gram(first, series, tables)
    gram, other = sum_over_space(partial, groups)
    counts = jnp.repeat(mode_count.reshape(GROUPS, PER), NROW, axis=1)
    modes, factor = modes_and_factor(gram, other, spectra, counts, all_points)
    return (modes.reshape(NFREQ, NROW, points_dev), factor)


def solution(mesh):
    in_specs = (P("space", "parts"), P(), P(), P())
    out_specs = (P(None, None, ("parts", "space")), P("parts", None, None))
    return jax.shard_map(
        on_device, mesh=mesh, in_specs=in_specs, out_specs=out_specs, check_vma=False
    )
```
